32 devices in a mesh: dap: 8 (over z, x), head: 4 (over y, core).
Axes of the slice: x: 2, y: 2, z: 4, core: 2. Of those that a mesh axis runs over, the one named last changes fastest.
Arguments:
- multiple_aligned_family: bfloat16 [128, 128, 256], P('dap')
- homolog_present_flags: int32 [128], replicated, may hold values from 0 to 1, as said below
- amino_present_flags: int32 [128], replicated, may hold values 0 or 1
- focus_layernorm_scaling: float32 [256], replicated, may hold values from 0.5 to 1.5
- focus_layernorm_offset: float32 [256], replicated, may hold values from -1.8 to 1.8
- combined_focus_matrices: bfloat16 [256, 4, 256], P(None, None, 'head')
- sigmoid_switch_offset: float32 [256], P('head'), may hold values from -4 to 4
- focus_final_matrix: bfloat16 [256, 256], P('head'), may hold values from -0.375 to 0.375
- focus_final_offset: float32 [256], replicated, may hold values from -3 to 3
- tensor_layernorm_scaling: float32 [256], replicated, may hold values from 0.5 to 1.5
- tensor_layernorm_offset: float32 [256], replicated, may hold values from -1.8 to 1.8
- tensor_product_factors: bfloat16 [256, 2, 32], replicated, may hold values from -0.375 to 0.375
- tensor_final_matrix: float32 [1024, 128], replicated, may hold values from -0.1875 to 0.1875
- tensor_final_offset: float32 [128], replicated, may hold values from -4 to 4
Outputs:
- alignment_output: bfloat16 [128, 128, 256], P(('dap', 'head'))
- pair_mean_update: float32 [128, 128, 128], P('dap', 'head')
The draws below stay inside these ranges and needn't reach their ends.
Inputs may be any that keep to these rules, and one draw needn't show every extreme that they name: homolog_present_flags[0] is always 1.
All inputs are finite; a program needn't handle non-finite values.
Results may differ from the reference program's by a relative error of at most 0.005.
Values may be sent and summed in bfloat16 or wider, within the bound.
A program may use at most 256 MiB of HBM per device.

```python
import math
import jax
import jax.numpy as jnp
from jax import lax

C = 256
H = 8
DH = 32
CZ = 128
CO = 32
RES_DEV = 16
S = 128
R = 128


def draw_multiple_aligned_family(key, part):
    keys = jax.random.split(jax.random.fold_in(key, 11), 3)
    profile = jax.random.normal(keys[0], (R, C), jnp.float32)
    noise = jax.random.normal(keys[1], (S, R, C), jnp.float32)
    seq_scale = jnp.exp(jax.random.uniform(keys[2], (S, 1, 1), jnp.float32, math.log(0.5), math.log(2.0)))
    mixed = profile[None] + noise * seq_scale
    return jnp.clip(mixed, -12.0, 12.0).astype(jnp.bfloat16)


def draw_combined_focus_matrices(key, part):
    keys = jax.random.split(jax.random.fold_in(key, 23), 1)
    weights = jax.random.normal(keys[0], (C, 4, H * DH), jnp.float32) * C ** (-0.5)
    return weights.astype(jnp.bfloat16)


def draw_homolog_present_flags(key, part):
    picks = jax.random.randint(jax.random.fold_in(key, 37), (S,), 0, 4)
    present = (picks > 0).astype(jnp.int32)
    return present.at[0].set(1)


def place_ends(values, rng, smallest, top_value):
    index_at = [jax.random.randint(jax.random.fold_in(rng, axis), (), 0, length) for axis, length in enumerate(values.shape)]
    main_axis = values.shape.index(max(values.shape))
    beside = index_at[:main_axis] + [(index_at[main_axis] + 1) % values.shape[main_axis]] + index_at[main_axis + 1:]
    return values.at[tuple(index_at)].set(smallest).at[tuple(beside)].set(top_value)


def block_scale(own_key, shape, cuts, low, top_value):
    level, own = 1.0, jax.random.fold_in(own_key, 6)
    for axis_at, blocks in cuts:
        heights = jnp.exp(jax.random.uniform(jax.random.fold_in(own, axis_at), (blocks,), jnp.float32, low / len(cuts), top_value / len(cuts)))
        level = level * jnp.repeat(heights, shape[axis_at] // blocks).reshape([-1 if axis == axis_at else 1 for axis in range(len(shape))])
    return level


def bell_draw(stream_key, extent, width, most, cuts=(), dtype=jnp.bfloat16):
    array = width * jax.random.normal(stream_key, extent, jnp.float32)
    if cuts:
        array = array * block_scale(stream_key, extent, cuts, -0.22, 0.18)
    return jnp.clip(array, -most, most).astype(dtype)


def setup_inputs(seed: int = 0) -> dict:
    streams_of = jax.random.split(jax.random.key(seed), 15)
    multiple_aligned_family = draw_multiple_aligned_family(jax.random.fold_in(streams_of[14], 71), 0)
    homolog_present_flags = draw_homolog_present_flags(jax.random.fold_in(streams_of[14], 71), 0)
    amino_present_flags = place_ends((jax.random.randint(streams_of[2], (R,), 0, 8) < 7).astype(jnp.int32), jax.random.fold_in(streams_of[2], 1), 0, 1)
    focus_layernorm_scaling = jnp.clip(1.0 + 0.1 * jax.random.normal(streams_of[3], (C,), jnp.float32), 0.5, 1.5)
    focus_layernorm_offset = bell_draw(streams_of[4], (C,), 0.3, 1.8, (), jnp.float32)
    combined_focus_matrices = draw_combined_focus_matrices(jax.random.fold_in(streams_of[14], 71), 0)
    sigmoid_switch_offset = bell_draw(streams_of[6], (H * DH,), 1.0, 4.0, ((0, 4),), jnp.float32)
    focus_final_matrix = bell_draw(streams_of[7], (H * DH, C), (H * DH) ** -0.5, 0.375, ((0, 4),))
    focus_final_offset = bell_draw(streams_of[8], (C,), 0.5, 3.0, (), jnp.float32)
    tensor_layernorm_scaling = jnp.clip(1.0 + 0.1 * jax.random.normal(streams_of[9], (C,), jnp.float32), 0.5, 1.5)
    tensor_layernorm_offset = bell_draw(streams_of[10], (C,), 0.3, 1.8, (), jnp.float32)
    tensor_product_factors = bell_draw(streams_of[11], (C, 2, CO), C ** -0.5, 0.375)
    tensor_final_matrix = bell_draw(streams_of[12], (CO * CO, CZ), (CO * CO) ** -0.5, 0.1875, (), jnp.float32)
    tensor_final_offset = bell_draw(streams_of[13], (CZ,), 1.0, 4.0, (), jnp.float32)
    return {"multiple_aligned_family": multiple_aligned_family, "homolog_present_flags": homolog_present_flags, "amino_present_flags": amino_present_flags, "focus_layernorm_scaling": focus_layernorm_scaling, "focus_layernorm_offset": focus_layernorm_offset, "combined_focus_matrices": combined_focus_matrices, "sigmoid_switch_offset": sigmoid_switch_offset, "focus_final_matrix": focus_final_matrix, "focus_final_offset": focus_final_offset, "tensor_layernorm_scaling": tensor_layernorm_scaling, "tensor_layernorm_offset": tensor_layernorm_offset, "tensor_product_factors": tensor_product_factors, "tensor_final_matrix": tensor_final_matrix, "tensor_final_offset": tensor_final_offset}


def layer_norm(value, gain, bias):
    mean = lax.optimization_barrier(jnp.mean(value, -1, keepdims=True))
    centred = value - mean
    spread = lax.optimization_barrier(jnp.mean(centred * centred, -1, keepdims=True))
    return centred * lax.rsqrt(spread + 1e-05) * gain + bias

def reference(multiple_aligned_family, homolog_present_flags, amino_present_flags, focus_layernorm_scaling, focus_layernorm_offset, combined_focus_matrices, sigmoid_switch_offset, focus_final_matrix, focus_final_offset, tensor_layernorm_scaling, tensor_layernorm_offset, tensor_product_factors, tensor_final_matrix, tensor_final_offset):
    keep = homolog_present_flags > 0
    weights_in = combined_focus_matrices.reshape(C, 4 * H * DH)
    gate_shift = sigmoid_switch_offset.reshape(H, DH)

    def lengthwise_portion(column_rows):
        normed = layer_norm(column_rows.astype(jnp.float32), focus_layernorm_scaling, focus_layernorm_offset).astype(jnp.bfloat16)
        projected = jnp.dot(normed, weights_in, preferred_element_type=jnp.float32).reshape(S, 4, H, DH)
        query = (projected[:, 0] * DH ** (-0.5)).astype(jnp.bfloat16)
        keys = projected[:, 1].astype(jnp.bfloat16)
        values = projected[:, 2].astype(jnp.bfloat16)
        gate = jax.nn.sigmoid(projected[:, 3] + gate_shift)
        scores = jnp.einsum('shd,thd->hst', query.astype(jnp.float32), keys.astype(jnp.float32))
        scores = jnp.where(keep[None, None, :], scores, jnp.float32(-1000000000.0))
        top = lax.optimization_barrier(jnp.max(scores, -1, keepdims=True))
        weights = jnp.exp(scores - top)
        probs = (weights / lax.optimization_barrier(jnp.sum(weights, -1, keepdims=True))).astype(jnp.bfloat16)
        mixed = jnp.einsum('hst,thd->shd', probs.astype(jnp.float32), values.astype(jnp.float32))
        attended = (mixed * gate).astype(jnp.bfloat16).reshape(S, H * DH)
        update = jnp.dot(attended, focus_final_matrix, preferred_element_type=jnp.float32)
        return (column_rows.astype(jnp.float32) + update + focus_final_offset).astype(jnp.bfloat16)
    refreshed_embedding = lax.map(lengthwise_portion, jnp.moveaxis(multiple_aligned_family, 1, 0))
    alignment_output = jnp.moveaxis(refreshed_embedding, 0, 1)
    opm_normed = layer_norm(refreshed_embedding.astype(jnp.float32), tensor_layernorm_scaling, tensor_layernorm_offset).astype(jnp.bfloat16)
    both = jnp.dot(opm_normed.reshape(R * S, C), tensor_product_factors.reshape(C, 2 * CO), preferred_element_type=jnp.float32).reshape(R, S, 2, CO)
    keep_rs = amino_present_flags.astype(jnp.float32)[:, None] * homolog_present_flags.astype(jnp.float32)[None, :]
    left = (both[:, :, 0] * keep_rs[:, :, None]).astype(jnp.bfloat16)
    right = (both[:, :, 1] * keep_rs[:, :, None]).astype(jnp.bfloat16)
    right_wide = right.astype(jnp.float32)

    def rows(left_block):
        outer = jnp.einsum('isc,jse->ijce', left_block.astype(jnp.float32), right_wide)
        flat = outer.reshape(RES_DEV * R, CO * CO)
        return jnp.dot(flat, tensor_final_matrix, precision=lax.Precision.HIGHEST, preferred_element_type=jnp.float32).reshape(RES_DEV, R, CZ)
    projected_pair = lax.map(rows, left.reshape(R // RES_DEV, RES_DEV, S, CO)).reshape(R, R, CZ)
    count = jnp.sum(homolog_present_flags).astype(jnp.float32)
    res_keep = amino_present_flags.astype(jnp.float32)
    norm = jnp.maximum(count * res_keep[:, None] * res_keep[None, :], 1.0)
    pair_mean_update = (projected_pair + tensor_final_offset) / norm[:, :, None]
    return (alignment_output, pair_mean_update)
```

```python
import functools

import jax
import jax.numpy as jnp
from jax import lax
from jax.experimental import pallas as pl
from jax.experimental.pallas import tpu as pltpu
from jax.sharding import PartitionSpec as P

DH = 32
CO = 32
F32 = jnp.float32
BF16 = jnp.bfloat16
MESH = pl.DeviceIdType.MESH


def dot(a, b, ca, cb, precision=None):
    return lax.dot_general(
        a, b, (((ca,), (cb,)), ((), ())), preferred_element_type=F32, precision=precision
    )


def iota(shape, dim):
    return lax.broadcasted_iota(jnp.int32, shape, dim)


def one_hot(hit):
    return jnp.where(hit, 1.0, 0.0).astype(BF16)


def layer_norm(value, gain, bias):
    mean = jnp.mean(value, -1, keepdims=True)
    centred = value - mean
    spread = jnp.mean(centred * centred, -1, keepdims=True)
    return centred * lax.rsqrt(spread + 1e-05) * gain + bias


def kernel(
    nd,
    nh,
    msa,
    homolog,
    amino,
    gain1,
    bias1,
    w_local,
    gate_local,
    wf_local,
    final_bias,
    gain2,
    bias2,
    factors,
    w_pair,
    pair_bias,
    align_out,
    pair_out,
    send1,
    recv1,
    w_all,
    wf_all,
    gate_col,
    gate_all,
    aligned,
    cbuf,
    crecv,
    lbuf,
    rstack,
    rbuf,
    left_all,
    right_all,
    w_r,
    obuf,
    s1,
    r1,
    s2,
    r2,
    s3,
    r3,
    s4,
    r4,
    s5,
    r5,
):
    md = lax.axis_index("dap")
    mh = lax.axis_index("head")
    sl, res, ch = msa.shape
    seqs = sl * nd
    rb = res // nd
    rd = rb // nh
    sg = sl // nh
    n = nd * nh
    hl = gate_local.shape[1]
    heads = hl * nh // DH
    dg = nd // nh
    ein = 16 // rd
    neb = CO // ein
    cz = w_pair.shape[1]
    me = md * nh + mh
    rows = rd * sl

    def peer(k):
        t = lax.rem(me + k, n)
        return t // nh, lax.rem(t, nh)

    barrier = pltpu.get_barrier_semaphore()
    for k in range(1, n):
        pl.semaphore_signal(barrier, inc=1, device_id=peer(k), device_id_type=MESH)

    ri = iota((rows, sl * rb), 0)
    ci = iota((rows, sl * rb), 1)
    pick = one_hot(ci == lax.rem(ri, sl) * rb + mh * rd + ri // sl)
    for d in range(nd):
        block = msa[:, d * rb : (d + 1) * rb, :].reshape(sl * rb, ch)
        send1[d] = dot(pick, block, 1, 0).astype(BF16)
    eye = jnp.where(iota((hl, hl), 0) == iota((hl, hl), 1), 1.0, 0.0).astype(F32)
    gate_col[...] = dot(
        eye, jnp.broadcast_to(gate_local[...], (128, hl)), 1, 1, lax.Precision.HIGHEST
    )
    pl.semaphore_wait(barrier, n - 1)

    copies = []

    def start(src, dst, ss, rs, to):
        c = pltpu.make_async_remote_copy(
            src_ref=src, dst_ref=dst, send_sem=ss, recv_sem=rs, device_id=to, device_id_type=MESH
        )
        c.start()
        copies.append(c)
        return c

    mine = pl.ds(pl.multiple_of(mh * hl, hl), hl)
    weights = []
    msas = []
    for k in range(1, nh):
        to = (md, lax.rem(mh + k, nh))
        weights.append(start(w_local, w_all.at[:, mine, :], s2.at[k, 0], r2.at[k, 0], to))
        weights.append(start(wf_local, wf_all.at[mine, :], s2.at[k, 1], r2.at[k, 1], to))
        weights.append(start(gate_col, gate_all.at[mine, :], s2.at[k, 2], r2.at[k, 2], to))
    for k in range(1, nd):
        to = lax.rem(md + k, nd)
        msas.append(start(send1.at[to], recv1.at[md], s1.at[k], r1.at[k], (to, mh)))

    recv1[md] = send1[md]
    w_all[:, mine, :] = w_local[...]
    wf_all[mine, :] = wf_local[...]
    gate_all[mine, :] = gate_col[...]
    for eb in range(neb):
        for e in range(ein):
            w_r[eb * CO : (eb + 1) * CO, e * cz : (e + 1) * cz] = w_pair[
                pl.ds(eb * ein + e, CO, stride=CO), :
            ].astype(BF16)
    seq_row = homolog[...].astype(F32)
    res_row = amino[...].astype(F32)
    count = jnp.sum(seq_row, axis=1, keepdims=True)
    seq_wide = jnp.broadcast_to(seq_row, (128, seqs)).astype(BF16)
    res_wide = jnp.broadcast_to(res_row, (128, res)).astype(BF16)
    seq_eye = one_hot(iota((seqs, seqs), 0) == iota((seqs, seqs), 1))
    seq_col = dot(seq_eye, seq_wide, 1, 1)[:, :1]
    penalty = jnp.broadcast_to(jnp.where(seq_col > 0.5, 0.0, -1e9), (seqs, seqs))
    own = one_hot(iota((8, res), 1) == md * rb + mh * rd + iota((8, res), 0))
    own_keep = dot(own, res_wide, 1, 1)[:, :1]
    for c in weights:
        c.wait_recv()
    for c in msas:
        c.wait_recv()

    for r in range(rd):
        x = recv1[:, r * sl : (r + 1) * sl, :].reshape(seqs, ch).astype(F32)
        normed = layer_norm(x, gain1[...], bias1[...]).astype(BF16)
        q = (dot(w_all[0], normed, 1, 1) * DH ** (-0.5)).astype(BF16)
        key = dot(w_all[1], normed, 1, 1).astype(BF16)
        val = dot(w_all[2], normed, 1, 1).astype(BF16)
        gate = jax.nn.sigmoid(dot(w_all[3], normed, 1, 1) + gate_all[:, :1])
        parts = []
        for h in range(heads):
            at = slice(h * DH, (h + 1) * DH)
            scores = dot(key[at], q[at], 0, 0) + penalty
            top = jnp.max(scores, 0, keepdims=True)
            w = jnp.exp(scores - top)
            total = jnp.sum(w, 0, keepdims=True)
            probs = (w * (1.0 / total)).astype(BF16)
            parts.append((dot(val[at], probs, 1, 0) * gate[at]).astype(BF16))
        attended = jnp.concatenate(parts, 0)
        update = dot(attended, wf_all[...], 0, 0)
        out = (x + update + final_bias[...]).astype(BF16)
        aligned[r] = out
        opm = layer_norm(out.astype(F32), gain2[...], bias2[...]).astype(BF16)
        both = dot(factors[...], opm, 1, 1) * (seq_row * own_keep[r : r + 1])
        lbuf[r * CO : (r + 1) * CO, :] = both[:CO].astype(BF16)
        rstack[r * CO : (r + 1) * CO, :] = both[CO:].astype(BF16)

    nr = rd * CO
    ri = iota((nr, nr), 0)
    mix = one_hot(iota((nr, nr), 1) == lax.rem(ri, rd) * CO + ri // rd)
    rbuf[...] = dot(mix, rstack[...], 1, 0).astype(BF16).reshape(rbuf.shape)
    to_h = md // dg
    slot = lax.rem(md, dg) * nh + mh
    spot = pl.ds(pl.multiple_of(slot * 16, 16), 16)

    def right_copy(k):
        return pltpu.make_async_remote_copy(
            src_ref=rbuf,
            dst_ref=right_all.at[:, spot, :],
            send_sem=s4.at[k],
            recv_sem=r4.at[slot],
            device_id=(lax.rem(md + k, nd), to_h),
            device_id_type=MESH,
        )

    @pl.when(to_h == mh)
    def _():
        right_all[:, spot, :] = rbuf[...]

    @pl.when(to_h != mh)
    def _():
        right_copy(0).start()

    for k in range(1, nd):
        right_copy(k).start()
    lefts = []
    for k in range(1, nh):
        to = (md, lax.rem(mh + k, nh))
        lefts.append(start(lbuf, left_all.at[mh], s5.at[k], r5.at[k], to))
    left_all[mh] = lbuf[...]

    ri = iota((rows, rows), 0)
    chunk = sg * rd
    col = lax.rem(ri, rd) * sl + (ri // chunk) * sg + lax.rem(ri, chunk) // rd
    order = one_hot(iota((rows, rows), 1) == col)
    for d in range(nd):
        block = aligned[:, d * sl : (d + 1) * sl, :].reshape(rows, ch)
        cbuf[d * nh : (d + 1) * nh] = dot(order, block, 1, 0).astype(BF16).reshape(nh, chunk, ch)
    outs = []
    for k in range(1, n):
        to = peer(k)
        outs.append(start(cbuf.at[lax.rem(me + k, n)], crecv.at[me], s3.at[k], r3.at[k], to))
    crecv[me] = cbuf[me]

    for c in lefts:
        c.wait_recv()
    for i in range(dg * nh):
        from_d = mh * dg + i // nh

        @pl.when(jnp.logical_or(from_d != md, i % nh != mh))
        def _():
            pltpu.make_async_remote_copy(
                src_ref=rbuf,
                dst_ref=right_all.at[:, i * 16 : (i + 1) * 16, :],
                send_sem=s4.at[0],
                recv_sem=r4.at[i],
                device_id=(md, to_h),
                device_id_type=MESH,
            ).wait_recv()

    left = left_all[...].reshape(nh * nr, seqs)
    for eb in range(neb):
        obuf[:, eb] = dot(left, right_all[eb], 1, 1).astype(BF16).reshape(rb, CO, -1)
    lanes = right_all.shape[1]
    cols = lanes // ein
    pick_i = one_hot(iota((rb, res), 1) == md * rb + iota((rb, res), 0))
    pick_j = one_hot(iota((cols, res), 1) == mh * cols + iota((cols, res), 0))
    keep_i = dot(pick_i, res_wide, 1, 1)[:, :cz]
    keep_j = dot(pick_j, res_wide, 1, 1)[:, :cz]
    group = lax.rem(iota((lanes, cz), 0), 16) // rd
    low = iota((8, cz), 0) < rd
    for i in range(rb):
        o = obuf[i].reshape(neb * CO, lanes)
        wide = dot(o, w_r[...], 0, 0)
        t = jnp.where(group == 0, wide[:, :cz], 0.0)
        for e in range(1, ein):
            t = jnp.where(group == e, wide[:, e * cz : (e + 1) * cz], t)
        t = t.reshape(lanes // 16, 2, 8, cz)
        u = t[:, 0] + t[:, 1]
        scale = 1.0 / jnp.maximum(count * keep_i[i : i + 1] * keep_j, 1.0)
        for g in range(cols // 8):
            a = u[2 * g]
            b = u[2 * g + 1]
            v = jnp.where(low, a + pltpu.roll(a, 4, 0), b + pltpu.roll(b, 4, 0))
            at = slice(g * 8, (g + 1) * 8)
            pair_out[i, at, :] = (v + pair_bias[...]) * scale[at]

    for c in outs:
        c.wait_recv()
    ri = iota((rows, rows), 0)
    wide_chunk = nh * rd
    col = lax.rem(ri, wide_chunk) // rd * chunk + ri // wide_chunk * rd + lax.rem(ri, rd)
    order = one_hot(iota((rows, rows), 1) == col)
    for d in range(nd):
        block = crecv[d * nh : (d + 1) * nh].reshape(rows, ch)
        align_out[:, d * rb : (d + 1) * rb, :] = (
            dot(order, block, 1, 0).astype(BF16).reshape(sg, rb, ch)
        )

    for c in copies:
        c.wait_send()

    @pl.when(to_h != mh)
    def _():
        right_copy(0).wait_send()

    for k in range(1, nd):
        right_copy(k).wait_send()


def per_device(
    nd,
    nh,
    multiple_aligned_family,
    homolog_present_flags,
    amino_present_flags,
    focus_layernorm_scaling,
    focus_layernorm_offset,
    combined_focus_matrices,
    sigmoid_switch_offset,
    focus_final_matrix,
    focus_final_offset,
    tensor_layernorm_scaling,
    tensor_layernorm_offset,
    tensor_product_factors,
    tensor_final_matrix,
    tensor_final_offset,
):
    sl, res, ch = multiple_aligned_family.shape
    seqs = homolog_present_flags.shape[0]
    hl = sigmoid_switch_offset.shape[0]
    cz = tensor_final_matrix.shape[1]
    rb = res // nd
    rd = rb // nh
    sg = sl // nh
    n = nd * nh
    ein = 16 // rd
    neb = CO // ein
    cols = res // nh
    row = lambda v: v.reshape(1, -1)
    w_local = combined_focus_matrices.transpose(1, 2, 0)
    factors = tensor_product_factors.transpose(1, 2, 0).reshape(2 * CO, ch)
    dma = pltpu.SemaphoreType.DMA
    vmem = pl.BlockSpec(memory_space=pltpu.VMEM)
    return pl.pallas_call(
        functools.partial(kernel, nd, nh),
        out_shape=(
            jax.ShapeDtypeStruct((sg, res, ch), BF16),
            jax.ShapeDtypeStruct((rb, cols, cz), F32),
        ),
        in_specs=[vmem] * 14,
        out_specs=(vmem, vmem),
        scratch_shapes=[
            pltpu.VMEM((nd, rd * sl, ch), BF16),
            pltpu.VMEM((nd, rd * sl, ch), BF16),
            pltpu.VMEM((4, nh * hl, ch), BF16),
            pltpu.VMEM((nh * hl, ch), BF16),
            pltpu.VMEM((hl, 128), F32),
            pltpu.VMEM((nh * hl, 128), F32),
            pltpu.VMEM((rd, seqs, ch), BF16),
            pltpu.VMEM((n, sg * rd, ch), BF16),
            pltpu.VMEM((n, sg * rd, ch), BF16),
            pltpu.VMEM((rd * CO, seqs), BF16),
            pltpu.VMEM((rd * CO, seqs), BF16),
            pltpu.VMEM((neb, 16, seqs), BF16),
            pltpu.VMEM((nh, rd * CO, seqs), BF16),
            pltpu.VMEM((neb, cols * ein, seqs), BF16),
            pltpu.VMEM((neb * CO, ein * cz), BF16),
            pltpu.VMEM((rb, neb, CO, cols * ein), BF16),
            dma((nd,)),
            dma((nd,)),
            dma((nh, 3)),
            dma((nh, 3)),
            dma((n,)),
            dma((n,)),
            dma((nd,)),
            dma((nd,)),
            dma((nh,)),
            dma((nh,)),
        ],
        compiler_params=pltpu.CompilerParams(
            collective_id=0, has_side_effects=True, vmem_limit_bytes=56 * 1024 * 1024
        ),
    )(
        multiple_aligned_family,
        row(homolog_present_flags),
        row(amino_present_flags),
        row(focus_layernorm_scaling),
        row(focus_layernorm_offset),
        w_local,
        row(sigmoid_switch_offset),
        focus_final_matrix,
        row(focus_final_offset),
        row(tensor_layernorm_scaling),
        row(tensor_layernorm_offset),
        factors,
        tensor_final_matrix,
        row(tensor_final_offset),
    )


def solution(mesh):
    nd = mesh.shape["dap"]
    nh = mesh.shape["head"]
    return jax.shard_map(
        functools.partial(per_device, nd, nh),
        mesh=mesh,
        in_specs=(
            P("dap", None, None),
            P(),
            P(),
            P(),
            P(),
            P(None, None, "head"),
            P("head"),
            P("head", None),
            P(),
            P(),
            P(),
            P(),
            P(),
            P(),
        ),
        out_specs=(P(("dap", "head"), None, None), P("dap", "head", None)),
        check_vma=False,
    )
```

```python
import functools

import jax
import jax.numpy as jnp
from jax import lax
from jax.experimental import pallas as pl
from jax.experimental.pallas import tpu as pltpu
from jax.sharding import PartitionSpec as P

DH = 32
CO = 32
F32 = jnp.float32
BF16 = jnp.bfloat16
MESH = pl.DeviceIdType.MESH


def dot(a, b, ca, cb, precision=None):
    return lax.dot_general(
        a, b, (((ca,), (cb,)), ((), ())), preferred_element_type=F32, precision=precision
    )


def iota(shape, dim):
    return lax.broadcasted_iota(jnp.int32, shape, dim)


def one_hot(hit):
    return jnp.where(hit, 1.0, 0.0).astype(BF16)


def layer_norm(value, gain, bias):
    mean = jnp.mean(value, -1, keepdims=True)
    centred = value - mean
    spread = jnp.mean(centred * centred, -1, keepdims=True)
    return centred * lax.rsqrt(spread + 1e-05) * gain + bias


def kernel(
    nd,
    nh,
    msa,
    homolog,
    amino,
    gain1,
    bias1,
    w_local,
    gate_local,
    wf_local,
    final_bias,
    gain2,
    bias2,
    factors,
    w_pair,
    pair_bias,
    align_out,
    pair_out,
    send1,
    recv1,
    w_all,
    wf_all,
    gate_rows,
    gate_all,
    aligned,
    cbuf,
    crecv,
    lbuf,
    rstack,
    right_in,
    left_all,
    right_all,
    w_r,
    obuf,
    s1,
    r1,
    s2,
    r2,
    s3,
    r3,
    s4,
    r4,
    s5,
    r5,
):
    md = lax.axis_index("dap")
    mh = lax.axis_index("head")
    sl, res, ch = msa.shape
    seqs = sl * nd
    rb = res // nd
    rd = rb // nh
    sg = sl // nh
    n = nd * nh
    hl = gate_local.shape[1]
    heads = hl * nh // DH
    dg = nd // nh
    ein = 16 // rd
    neb = CO // ein
    cz = w_pair.shape[1]
    me = md * nh + mh
    rows = rd * sl

    def peer(k):
        t = lax.rem(me + k, n)
        return t // nh, lax.rem(t, nh)

    barrier = pltpu.get_barrier_semaphore()
    partner = mh + 1 - 2 * lax.rem(mh, 2)
    for k in range(1, nh):
        to = (md, lax.rem(mh + k, nh))
        pl.semaphore_signal(barrier, inc=1, device_id=to, device_id_type=MESH)
    for k in range(1, nd):
        to = (lax.rem(md + k, nd), mh)
        pl.semaphore_signal(barrier, inc=1, device_id=to, device_id_type=MESH)

    ri = iota((rows, sl * rb), 0)
    ci = iota((rows, sl * rb), 1)
    pick = one_hot(ci == lax.rem(ri, sl) * rb + mh * rd + ri // sl)
    for d in range(nd):
        block = msa[:, d * rb : (d + 1) * rb, :].reshape(sl * rb, ch)
        send1[d] = dot(pick, block, 1, 0).astype(BF16)
    pl.semaphore_wait(barrier, nd + nh - 2)

    copies = []

    def start(src, dst, ss, rs, to):
        c = pltpu.make_async_remote_copy(
            src_ref=src, dst_ref=dst, send_sem=ss, recv_sem=rs, device_id=to, device_id_type=MESH
        )
        c.start()
        copies.append(c)
        return c

    def head_rows(g):
        return pl.ds(pl.multiple_of(g * hl, hl), hl)

    def send_weights(g, own, idx, to):
        at = head_rows(g)
        src = (
            (w_local, wf_local, gate_local)
            if own
            else (w_all.at[:, at, :], wf_all.at[at, :], gate_rows.at[g])
        )
        dst = (w_all.at[:, at, :], wf_all.at[at, :], gate_rows.at[g])
        for j in range(3):
            start(src[j], dst[j], s2.at[idx, j], r2.at[g, j], (md, to))

    def wait_weights(g):
        at = head_rows(g)
        src = (w_local, wf_local, gate_local)
        dst = (w_all.at[:, at, :], wf_all.at[at, :], gate_rows.at[g])
        for j in range(3):
            pltpu.make_async_remote_copy(
                src_ref=src[j],
                dst_ref=dst[j],
                send_sem=s2.at[0, j],
                recv_sem=r2.at[g, j],
                device_id=(md, partner),
                device_id_type=MESH,
            ).wait_recv()

    mine = head_rows(mh)
    pairs = nh // 2
    for k in range(1, pairs):
        send_weights(mh, True, k, lax.rem(mh + 2 * k, nh))
    send_weights(mh, True, 0, partner)
    msas = []
    for r in range(rd):
        at = slice(r * sl, (r + 1) * sl)
        for k in range(1, nd):
            to = lax.rem(md + k, nd)
            msas.append(
                start(send1.at[to, at], recv1.at[md, at], s1.at[k, r], r1.at[k, r], (to, mh))
            )

    recv1[md] = send1[md]
    w_all[:, mine, :] = w_local[...]
    wf_all[mine, :] = wf_local[...]
    gate_rows[mh] = gate_local[...]
    for eb in range(neb):
        for e in range(ein):
            w_r[eb * CO : (eb + 1) * CO, e * cz : (e + 1) * cz] = w_pair[
                pl.ds(eb * ein + e, CO, stride=CO), :
            ].astype(BF16)
    seq_row = homolog[...].astype(F32)
    res_row = amino[...].astype(F32)
    count = jnp.sum(seq_row, axis=1, keepdims=True)
    seq_wide = jnp.broadcast_to(seq_row, (128, seqs)).astype(BF16)
    res_wide = jnp.broadcast_to(res_row, (128, res)).astype(BF16)
    seq_eye = one_hot(iota((seqs, seqs), 0) == iota((seqs, seqs), 1))
    seq_col = dot(seq_eye, seq_wide, 1, 1)[:, :1]
    penalty = jnp.broadcast_to(jnp.where(seq_col > 0.5, 0.0, -1e9), (seqs, seqs))
    own = one_hot(iota((8, res), 1) == md * rb + mh * rd + iota((8, res), 0))
    own_keep = dot(own, res_wide, 1, 1)[:, :1]
    for k in range(1, pairs):
        g = lax.rem(mh + nh - 2 * k, nh)
        wait_weights(g)
        send_weights(g, False, pairs - 1 + k, partner)
    wait_weights(partner)
    for k in range(1, pairs):
        wait_weights(lax.rem(partner + nh - 2 * k, nh))
    eye = jnp.where(iota((hl, hl), 0) == iota((hl, hl), 1), 1.0, 0.0).astype(F32)
    for g in range(nh):
        wide = jnp.broadcast_to(gate_rows[g], (128, hl))
        gate_all[g * hl : (g + 1) * hl, :] = dot(eye, wide, 1, 1, lax.Precision.HIGHEST)

    to_h = md // dg
    slot = lax.rem(md, dg) * nh + mh

    def right_copy(k, r, i):
        at = slice(r * CO, (r + 1) * CO)
        return pltpu.make_async_remote_copy(
            src_ref=rstack.at[at, :],
            dst_ref=right_in.at[i, at, :],
            send_sem=s4.at[k, r],
            recv_sem=r4.at[i, r],
            device_id=(lax.rem(md + k, nd), to_h),
            device_id_type=MESH,
        )

    lefts = []

    for r in range(rd):
        for c in msas[r * (nd - 1) : (r + 1) * (nd - 1)]:
            c.wait_recv()
        x = recv1[:, r * sl : (r + 1) * sl, :].reshape(seqs, ch).astype(F32)
        normed = layer_norm(x, gain1[...], bias1[...]).astype(BF16)
        q = (dot(w_all[0], normed, 1, 1) * DH ** (-0.5)).astype(BF16)
        key = dot(w_all[1], normed, 1, 1).astype(BF16)
        val = dot(w_all[2], normed, 1, 1).astype(BF16)
        gate = jax.nn.sigmoid(dot(w_all[3], normed, 1, 1) + gate_all[:, :1])
        parts = []
        for h in range(heads):
            at = slice(h * DH, (h + 1) * DH)
            scores = dot(key[at], q[at], 0, 0) + penalty
            top = jnp.max(scores, 0, keepdims=True)
            w = jnp.exp(scores - top)
            total = jnp.sum(w, 0, keepdims=True)
            probs = (w * (1.0 / total)).astype(BF16)
            parts.append((dot(val[at], probs, 1, 0) * gate[at]).astype(BF16))
        attended = jnp.concatenate(parts, 0)
        update = dot(attended, wf_all[...], 0, 0)
        out = (x + update + final_bias[...]).astype(BF16)
        aligned[r] = out
        opm = layer_norm(out.astype(F32), gain2[...], bias2[...]).astype(BF16)
        both = dot(factors[...], opm, 1, 1) * (seq_row * own_keep[r : r + 1])
        lbuf[r * CO : (r + 1) * CO, :] = both[:CO].astype(BF16)
        rstack[r * CO : (r + 1) * CO, :] = both[CO:].astype(BF16)

        at = slice(r * CO, (r + 1) * CO)

        @pl.when(to_h != mh)
        def _():
            right_copy(0, r, slot).start()

        for k in range(1, nd):
            right_copy(k, r, slot).start()
        for k in range(1, nh):
            to = (md, lax.rem(mh + k, nh))
            lefts.append(
                start(lbuf.at[at, :], left_all.at[mh, at, :], s5.at[k, r], r5.at[k, r], to)
            )

    @pl.when(to_h == mh)
    def _():
        right_in[slot] = rstack[...]

    left_all[mh] = lbuf[...]

    ri = iota((rows, rows), 0)
    chunk = sg * rd
    col = lax.rem(ri, rd) * sl + (ri // chunk) * sg + lax.rem(ri, chunk) // rd
    order = one_hot(iota((rows, rows), 1) == col)
    for d in range(nd):
        block = aligned[:, d * sl : (d + 1) * sl, :].reshape(rows, ch)
        cbuf[d * nh : (d + 1) * nh] = dot(order, block, 1, 0).astype(BF16).reshape(nh, chunk, ch)
    outs = []
    for k in range(1, n):
        to = peer(k)
        outs.append(start(cbuf.at[lax.rem(me + k, n)], crecv.at[me], s3.at[k], r3.at[k], to))
    crecv[me] = cbuf[me]

    for c in lefts:
        c.wait_recv()
    nr = rd * CO
    ri = iota((nr, nr), 0)
    mix = one_hot(iota((nr, nr), 1) == lax.rem(ri, rd) * CO + ri // rd)
    for i in range(dg * nh):
        from_d = mh * dg + i // nh

        @pl.when(jnp.logical_or(from_d != md, i % nh != mh))
        def _():
            for r in range(rd):
                right_copy(0, r, i).wait_recv()

        part = dot(mix, right_in[i], 1, 0).astype(BF16)
        right_all[:, i * 16 : (i + 1) * 16, :] = part.reshape(neb, 16, seqs)

    left = left_all[...].reshape(nh * nr, seqs)
    for eb in range(neb):
        obuf[:, eb] = dot(left, right_all[eb], 1, 1).astype(BF16).reshape(rb, CO, -1)
    lanes = right_all.shape[1]
    cols = lanes // ein
    pick_i = one_hot(iota((rb, res), 1) == md * rb + iota((rb, res), 0))
    pick_j = one_hot(iota((cols, res), 1) == mh * cols + iota((cols, res), 0))
    keep_i = dot(pick_i, res_wide, 1, 1)[:, :cz]
    keep_j = dot(pick_j, res_wide, 1, 1)[:, :cz]
    group = lax.rem(iota((lanes, cz), 0), 16) // rd
    low = iota((8, cz), 0) < rd
    for i in range(rb):
        o = obuf[i].reshape(neb * CO, lanes)
        wide = dot(o, w_r[...], 0, 0)
        t = jnp.where(group == 0, wide[:, :cz], 0.0)
        for e in range(1, ein):
            t = jnp.where(group == e, wide[:, e * cz : (e + 1) * cz], t)
        t = t.reshape(lanes // 16, 2, 8, cz)
        u = t[:, 0] + t[:, 1]
        scale = 1.0 / jnp.maximum(count * keep_i[i : i + 1] * keep_j, 1.0)
        for g in range(cols // 8):
            a = u[2 * g]
            b = u[2 * g + 1]
            v = jnp.where(low, a + pltpu.roll(a, 4, 0), b + pltpu.roll(b, 4, 0))
            at = slice(g * 8, (g + 1) * 8)
            pair_out[i, at, :] = (v + pair_bias[...]) * scale[at]

    for c in outs:
        c.wait_recv()
    ri = iota((rows, rows), 0)
    wide_chunk = nh * rd
    col = lax.rem(ri, wide_chunk) // rd * chunk + ri // wide_chunk * rd + lax.rem(ri, rd)
    order = one_hot(iota((rows, rows), 1) == col)
    for d in range(nd):
        block = crecv[d * nh : (d + 1) * nh].reshape(rows, ch)
        align_out[:, d * rb : (d + 1) * rb, :] = (
            dot(order, block, 1, 0).astype(BF16).reshape(sg, rb, ch)
        )

    for c in copies:
        c.wait_send()

    for r in range(rd):

        @pl.when(to_h != mh)
        def _():
            right_copy(0, r, slot).wait_send()

        for k in range(1, nd):
            right_copy(k, r, slot).wait_send()


def per_device(
    nd,
    nh,
    multiple_aligned_family,
    homolog_present_flags,
    amino_present_flags,
    focus_layernorm_scaling,
    focus_layernorm_offset,
    combined_focus_matrices,
    sigmoid_switch_offset,
    focus_final_matrix,
    focus_final_offset,
    tensor_layernorm_scaling,
    tensor_layernorm_offset,
    tensor_product_factors,
    tensor_final_matrix,
    tensor_final_offset,
):
    sl, res, ch = multiple_aligned_family.shape
    seqs = homolog_present_flags.shape[0]
    hl = sigmoid_switch_offset.shape[0]
    cz = tensor_final_matrix.shape[1]
    rb = res // nd
    rd = rb // nh
    sg = sl // nh
    n = nd * nh
    ein = 16 // rd
    neb = CO // ein
    cols = res // nh
    row = lambda v: v.reshape(1, -1)
    w_local = combined_focus_matrices.transpose(1, 2, 0)
    factors = tensor_product_factors.transpose(1, 2, 0).reshape(2 * CO, ch)
    dma = pltpu.SemaphoreType.DMA
    vmem = pl.BlockSpec(memory_space=pltpu.VMEM)
    return pl.pallas_call(
        functools.partial(kernel, nd, nh),
        out_shape=(
            jax.ShapeDtypeStruct((sg, res, ch), BF16),
            jax.ShapeDtypeStruct((rb, cols, cz), F32),
        ),
        in_specs=[vmem] * 14,
        out_specs=(vmem, vmem),
        scratch_shapes=[
            pltpu.VMEM((nd, rd * sl, ch), BF16),
            pltpu.VMEM((nd, rd * sl, ch), BF16),
            pltpu.VMEM((4, nh * hl, ch), BF16),
            pltpu.VMEM((nh * hl, ch), BF16),
            pltpu.VMEM((nh, 1, hl), F32),
            pltpu.VMEM((nh * hl, 128), F32),
            pltpu.VMEM((rd, seqs, ch), BF16),
            pltpu.VMEM((n, sg * rd, ch), BF16),
            pltpu.VMEM((n, sg * rd, ch), BF16),
            pltpu.VMEM((rd * CO, seqs), BF16),
            pltpu.VMEM((rd * CO, seqs), BF16),
            pltpu.VMEM((nd, rd * CO, seqs), BF16),
            pltpu.VMEM((nh, rd * CO, seqs), BF16),
            pltpu.VMEM((neb, cols * ein, seqs), BF16),
            pltpu.VMEM((neb * CO, ein * cz), BF16),
            pltpu.VMEM((rb, neb, CO, cols * ein), BF16),
            dma((nd, rd)),
            dma((nd, rd)),
            dma((nh, 3)),
            dma((nh, 3)),
            dma((n,)),
            dma((n,)),
            dma((nd, rd)),
            dma((nd, rd)),
            dma((nh, rd)),
            dma((nh, rd)),
        ],
        compiler_params=pltpu.CompilerParams(
            collective_id=0, has_side_effects=True, vmem_limit_bytes=56 * 1024 * 1024
        ),
    )(
        multiple_aligned_family,
        row(homolog_present_flags),
        row(amino_present_flags),
        row(focus_layernorm_scaling),
        row(focus_layernorm_offset),
        w_local,
        row(sigmoid_switch_offset),
        focus_final_matrix,
        row(focus_final_offset),
        row(tensor_layernorm_scaling),
        row(tensor_layernorm_offset),
        factors,
        tensor_final_matrix,
        row(tensor_final_offset),
    )


def solution(mesh):
    nd = mesh.shape["dap"]
    nh = mesh.shape["head"]
    return jax.shard_map(
        functools.partial(per_device, nd, nh),
        mesh=mesh,
        in_specs=(
            P("dap", None, None),
            P(),
            P(),
            P(),
            P(),
            P(None, None, "head"),
            P("head"),
            P("head", None),
            P(),
            P(),
            P(),
            P(),
            P(),
            P(),
        ),
        out_specs=(P(("dap", "head"), None, None), P("dap", "head", None)),
        check_vma=False,
    )
```

```python
import functools

import jax
import jax.numpy as jnp
from jax import lax
from jax.experimental import pallas as pl
from jax.experimental.pallas import tpu as pltpu
from jax.sharding import PartitionSpec as P

DH = 32
CO = 32
F32 = jnp.float32
BF16 = jnp.bfloat16
MESH = pl.DeviceIdType.MESH


def dot(a, b, ca, cb, precision=None):
    return lax.dot_general(
        a, b, (((ca,), (cb,)), ((), ())), preferred_element_type=F32, precision=precision
    )


def iota(shape, dim):
    return lax.broadcasted_iota(jnp.int32, shape, dim)


def one_hot(hit):
    return jnp.where(hit, 1.0, 0.0).astype(BF16)


def layer_norm(value, gain, bias):
    mean = jnp.mean(value, -1, keepdims=True)
    centred = value - mean
    spread = jnp.mean(centred * centred, -1, keepdims=True)
    return centred * lax.rsqrt(spread + 1e-05) * gain + bias


def kernel(
    nd,
    nh,
    *refs,
):
    args = refs[:14]
    align_out, pair_out = refs[14:16]
    held = refs[16:30]
    (
        msa,
        homolog,
        amino,
        gain1,
        bias1,
        w_local,
        gate_local,
        wf_local,
        final_bias,
        gain2,
        bias2,
        factors,
        w_pair,
        pair_bias,
    ) = held
    (
        load_sem,
        send1,
        recv1,
        w_all,
        wf_all,
        gate_rows,
        gate_all,
        aligned,
        cbuf,
        crecv,
        lbuf,
        rstack,
        right_in,
        left_all,
        right_all,
        w_r,
        obuf,
        s1,
        r1,
        s2,
        r2,
        s3,
        r3,
        s4,
        r4,
        s5,
        r5,
    ) = refs[30:]
    md = lax.axis_index("dap")
    mh = lax.axis_index("head")
    sl, res, ch = msa.shape
    seqs = sl * nd
    rb = res // nd
    rd = rb // nh
    sg = sl // nh
    n = nd * nh
    hl = gate_local.shape[1]
    heads = hl * nh // DH
    dg = nd // nh
    ein = 16 // rd
    neb = CO // ein
    cz = w_pair.shape[1]
    me = md * nh + mh
    rows = rd * sl

    def peer(k):
        t = lax.rem(me + k, n)
        return t // nh, lax.rem(t, nh)

    barrier = pltpu.get_barrier_semaphore()
    partner = mh + 1 - 2 * lax.rem(mh, 2)
    for k in range(1, nh):
        to = (md, lax.rem(mh + k, nh))
        pl.semaphore_signal(barrier, inc=1, device_id=to, device_id_type=MESH)
    for k in range(1, nd):
        to = (lax.rem(md + k, nd), mh)
        pl.semaphore_signal(barrier, inc=1, device_id=to, device_id_type=MESH)

    loads = [pltpu.make_async_copy(args[i], held[i], load_sem.at[i]) for i in range(14)]
    for c in loads:
        c.start()
    loads[0].wait()

    ri = iota((rows, sl * rb), 0)
    ci = iota((rows, sl * rb), 1)
    pick = one_hot(ci == lax.rem(ri, sl) * rb + mh * rd + ri // sl)
    for d in range(nd):
        block = msa[:, d * rb : (d + 1) * rb, :].reshape(sl * rb, ch)
        send1[d] = dot(pick, block, 1, 0).astype(BF16)
    for c in loads[1:]:
        c.wait()
    for eb in range(neb):
        for e in range(ein):
            w_r[eb * CO : (eb + 1) * CO, e * cz : (e + 1) * cz] = w_pair[
                pl.ds(eb * ein + e, CO, stride=CO), :
            ].astype(BF16)
    seq_row = homolog[...].astype(F32)
    res_row = amino[...].astype(F32)
    count = jnp.sum(seq_row, axis=1, keepdims=True)
    seq_wide = jnp.broadcast_to(seq_row, (128, seqs)).astype(BF16)
    res_wide = jnp.broadcast_to(res_row, (128, res)).astype(BF16)
    seq_eye = one_hot(iota((seqs, seqs), 0) == iota((seqs, seqs), 1))
    seq_col = dot(seq_eye, seq_wide, 1, 1)[:, :1]
    penalty = jnp.broadcast_to(jnp.where(seq_col > 0.5, 0.0, -1e9), (seqs, seqs))
    own = one_hot(iota((8, res), 1) == md * rb + mh * rd + iota((8, res), 0))
    own_keep = dot(own, res_wide, 1, 1)[:, :1]
    pl.semaphore_wait(barrier, nd + nh - 2)

    copies = []

    def start(src, dst, ss, rs, to):
        c = pltpu.make_async_remote_copy(
            src_ref=src, dst_ref=dst, send_sem=ss, recv_sem=rs, device_id=to, device_id_type=MESH
        )
        c.start()
        copies.append(c)
        return c

    def head_rows(g):
        return pl.ds(pl.multiple_of(g * hl, hl), hl)

    def send_weights(g, own, idx, to):
        at = head_rows(g)
        src = (
            (w_local, wf_local, gate_local)
            if own
            else (w_all.at[:, at, :], wf_all.at[at, :], gate_rows.at[g])
        )
        dst = (w_all.at[:, at, :], wf_all.at[at, :], gate_rows.at[g])
        for j in range(3):
            start(src[j], dst[j], s2.at[idx, j], r2.at[g, j], (md, to))

    def wait_weights(g):
        at = head_rows(g)
        src = (w_local, wf_local, gate_local)
        dst = (w_all.at[:, at, :], wf_all.at[at, :], gate_rows.at[g])
        for j in range(3):
            pltpu.make_async_remote_copy(
                src_ref=src[j],
                dst_ref=dst[j],
                send_sem=s2.at[0, j],
                recv_sem=r2.at[g, j],
                device_id=(md, partner),
                device_id_type=MESH,
            ).wait_recv()

    mine = head_rows(mh)
    pairs = nh // 2
    for k in range(1, pairs):
        send_weights(mh, True, k, lax.rem(mh + 2 * k, nh))
    send_weights(mh, True, 0, partner)
    msas = []
    for r in range(rd):
        at = slice(r * sl, (r + 1) * sl)
        for k in range(1, nd):
            to = lax.rem(md + k, nd)
            msas.append(
                start(send1.at[to, at], recv1.at[md, at], s1.at[k, r], r1.at[k, r], (to, mh))
            )

    recv1[md] = send1[md]
    w_all[:, mine, :] = w_local[...]
    wf_all[mine, :] = wf_local[...]
    gate_rows[mh] = gate_local[...]
    for k in range(1, pairs):
        g = lax.rem(mh + nh - 2 * k, nh)
        wait_weights(g)
        send_weights(g, False, pairs - 1 + k, partner)
    wait_weights(partner)
    for k in range(1, pairs):
        wait_weights(lax.rem(partner + nh - 2 * k, nh))
    eye = jnp.where(iota((hl, hl), 0) == iota((hl, hl), 1), 1.0, 0.0).astype(F32)
    for g in range(nh):
        wide = jnp.broadcast_to(gate_rows[g], (128, hl))
        gate_all[g * hl : (g + 1) * hl, :] = dot(eye, wide, 1, 1, lax.Precision.HIGHEST)

    to_h = md // dg
    slot = lax.rem(md, dg) * nh + mh

    def right_copy(k, r, i):
        at = slice(r * CO, (r + 1) * CO)
        return pltpu.make_async_remote_copy(
            src_ref=rstack.at[at, :],
            dst_ref=right_in.at[i, at, :],
            send_sem=s4.at[k, r],
            recv_sem=r4.at[i, r],
            device_id=(lax.rem(md + k, nd), to_h),
            device_id_type=MESH,
        )

    lefts = []

    for r in range(rd):
        for c in msas[r * (nd - 1) : (r + 1) * (nd - 1)]:
            c.wait_recv()
        x = recv1[:, r * sl : (r + 1) * sl, :].reshape(seqs, ch).astype(F32)
        normed = layer_norm(x, gain1[...], bias1[...]).astype(BF16)
        q = (dot(w_all[0], normed, 1, 1) * DH ** (-0.5)).astype(BF16)
        key = dot(w_all[1], normed, 1, 1).astype(BF16)
        val = dot(w_all[2], normed, 1, 1).astype(BF16)
        gate = jax.nn.sigmoid(dot(w_all[3], normed, 1, 1) + gate_all[:, :1])
        ats = [slice(h * DH, (h + 1) * DH) for h in range(heads)]
        scores = [dot(key[at], q[at], 0, 0) + penalty for at in ats]
        tops = [jnp.max(v, 0, keepdims=True) for v in scores]
        ws = [jnp.exp(v - top) for v, top in zip(scores, tops)]
        totals = [1.0 / jnp.sum(w, 0, keepdims=True) for w in ws]
        probs = [(w * t).astype(BF16) for w, t in zip(ws, totals)]
        parts = [(dot(val[at], p, 1, 0) * gate[at]).astype(BF16) for at, p in zip(ats, probs)]
        attended = jnp.concatenate(parts, 0)
        update = dot(attended, wf_all[...], 0, 0)
        out = (x + update + final_bias[...]).astype(BF16)
        aligned[r] = out
        opm = layer_norm(out.astype(F32), gain2[...], bias2[...]).astype(BF16)
        both = dot(factors[...], opm, 1, 1) * (seq_row * own_keep[r : r + 1])
        lbuf[r * CO : (r + 1) * CO, :] = both[:CO].astype(BF16)
        rstack[r * CO : (r + 1) * CO, :] = both[CO:].astype(BF16)

        at = slice(r * CO, (r + 1) * CO)

        @pl.when(to_h != mh)
        def _():
            right_copy(0, r, slot).start()

        for k in range(1, nd):
            right_copy(k, r, slot).start()
        for k in range(1, nh):
            to = (md, lax.rem(mh + k, nh))
            lefts.append(
                start(lbuf.at[at, :], left_all.at[mh, at, :], s5.at[k, r], r5.at[k, r], to)
            )

    @pl.when(to_h == mh)
    def _():
        right_in[slot] = rstack[...]

    left_all[mh] = lbuf[...]

    ri = iota((rows, rows), 0)
    chunk = sg * rd
    col = lax.rem(ri, rd) * sl + (ri // chunk) * sg + lax.rem(ri, chunk) // rd
    order = one_hot(iota((rows, rows), 1) == col)
    for d in range(nd):
        block = aligned[:, d * sl : (d + 1) * sl, :].reshape(rows, ch)
        cbuf[d * nh : (d + 1) * nh] = dot(order, block, 1, 0).astype(BF16).reshape(nh, chunk, ch)
    outs = []
    for k in range(1, n):
        to = peer(k)
        outs.append(start(cbuf.at[lax.rem(me + k, n)], crecv.at[me], s3.at[k], r3.at[k], to))
    crecv[me] = cbuf[me]

    for c in lefts:
        c.wait_recv()
    nr = rd * CO
    ri = iota((nr, nr), 0)
    mix = one_hot(iota((nr, nr), 1) == lax.rem(ri, rd) * CO + ri // rd)
    for i in range(dg * nh):
        from_d = mh * dg + i // nh

        @pl.when(jnp.logical_or(from_d != md, i % nh != mh))
        def _():
            for r in range(rd):
                right_copy(0, r, i).wait_recv()

        part = dot(mix, right_in[i], 1, 0).astype(BF16)
        right_all[:, i * 16 : (i + 1) * 16, :] = part.reshape(neb, 16, seqs)

    left = left_all[...].reshape(nh * nr, seqs)
    for eb in range(neb):
        obuf[:, eb] = dot(left, right_all[eb], 1, 1).astype(BF16).reshape(rb, CO, -1)
    lanes = right_all.shape[1]
    cols = lanes // ein
    pick_i = one_hot(iota((rb, res), 1) == md * rb + iota((rb, res), 0))
    pick_j = one_hot(iota((cols, res), 1) == mh * cols + iota((cols, res), 0))
    keep_i = dot(pick_i, res_wide, 1, 1)[:, :cz]
    keep_j = dot(pick_j, res_wide, 1, 1)[:, :cz]
    group = lax.rem(iota((lanes, cz), 0), 16) // rd
    low = iota((8, cz), 0) < rd
    for i in range(rb):
        o = obuf[i].reshape(neb * CO, lanes)
        wide = dot(o, w_r[...], 0, 0)
        t = jnp.where(group == 0, wide[:, :cz], 0.0)
        for e in range(1, ein):
            t = jnp.where(group == e, wide[:, e * cz : (e + 1) * cz], t)
        t = t.reshape(lanes // 16, 2, 8, cz)
        u = t[:, 0] + t[:, 1]
        scale = 1.0 / jnp.maximum(count * keep_i[i : i + 1] * keep_j, 1.0)
        for g in range(cols // 8):
            a = u[2 * g]
            b = u[2 * g + 1]
            v = jnp.where(low, a + pltpu.roll(a, 4, 0), b + pltpu.roll(b, 4, 0))
            at = slice(g * 8, (g + 1) * 8)
            pair_out[i, at, :] = (v + pair_bias[...]) * scale[at]

    for c in outs:
        c.wait_recv()
    ri = iota((rows, rows), 0)
    wide_chunk = nh * rd
    col = lax.rem(ri, wide_chunk) // rd * chunk + ri // wide_chunk * rd + lax.rem(ri, rd)
    order = one_hot(iota((rows, rows), 1) == col)
    for d in range(nd):
        block = crecv[d * nh : (d + 1) * nh].reshape(rows, ch)
        align_out[:, d * rb : (d + 1) * rb, :] = (
            dot(order, block, 1, 0).astype(BF16).reshape(sg, rb, ch)
        )

    for c in copies:
        c.wait_send()

    for r in range(rd):

        @pl.when(to_h != mh)
        def _():
            right_copy(0, r, slot).wait_send()

        for k in range(1, nd):
            right_copy(k, r, slot).wait_send()


def per_device(
    nd,
    nh,
    multiple_aligned_family,
    homolog_present_flags,
    amino_present_flags,
    focus_layernorm_scaling,
    focus_layernorm_offset,
    combined_focus_matrices,
    sigmoid_switch_offset,
    focus_final_matrix,
    focus_final_offset,
    tensor_layernorm_scaling,
    tensor_layernorm_offset,
    tensor_product_factors,
    tensor_final_matrix,
    tensor_final_offset,
):
    sl, res, ch = multiple_aligned_family.shape
    seqs = homolog_present_flags.shape[0]
    hl = sigmoid_switch_offset.shape[0]
    cz = tensor_final_matrix.shape[1]
    rb = res // nd
    rd = rb // nh
    sg = sl // nh
    n = nd * nh
    ein = 16 // rd
    neb = CO // ein
    cols = res // nh
    row = lambda v: v.reshape(1, -1)
    w_local = combined_focus_matrices.transpose(1, 2, 0)
    factors = tensor_product_factors.transpose(1, 2, 0).reshape(2 * CO, ch)
    dma = pltpu.SemaphoreType.DMA
    vmem = pl.BlockSpec(memory_space=pltpu.VMEM)
    operands = (
        multiple_aligned_family,
        row(homolog_present_flags),
        row(amino_present_flags),
        row(focus_layernorm_scaling),
        row(focus_layernorm_offset),
        w_local,
        row(sigmoid_switch_offset),
        focus_final_matrix,
        row(focus_final_offset),
        row(tensor_layernorm_scaling),
        row(tensor_layernorm_offset),
        factors,
        tensor_final_matrix,
        row(tensor_final_offset),
    )
    return pl.pallas_call(
        functools.partial(kernel, nd, nh),
        out_shape=(
            pltpu.VMEM((sg, res, ch), BF16),
            pltpu.VMEM((rb, cols, cz), F32),
        ),
        in_specs=[pl.BlockSpec(memory_space=pl.ANY)] * 14,
        out_specs=(vmem, vmem),
        scratch_shapes=[pltpu.VMEM(v.shape, v.dtype) for v in operands]
        + [
            dma((14,)),
            pltpu.VMEM((nd, rd * sl, ch), BF16),
            pltpu.VMEM((nd, rd * sl, ch), BF16),
            pltpu.VMEM((4, nh * hl, ch), BF16),
            pltpu.VMEM((nh * hl, ch), BF16),
            pltpu.VMEM((nh, 1, hl), F32),
            pltpu.VMEM((nh * hl, 128), F32),
            pltpu.VMEM((rd, seqs, ch), BF16),
            pltpu.VMEM((n, sg * rd, ch), BF16),
            pltpu.VMEM((n, sg * rd, ch), BF16),
            pltpu.VMEM((rd * CO, seqs), BF16),
            pltpu.VMEM((rd * CO, seqs), BF16),
            pltpu.VMEM((nd, rd * CO, seqs), BF16),
            pltpu.VMEM((nh, rd * CO, seqs), BF16),
            pltpu.VMEM((neb, cols * ein, seqs), BF16),
            pltpu.VMEM((neb * CO, ein * cz), BF16),
            pltpu.VMEM((rb, neb, CO, cols * ein), BF16),
            dma((nd, rd)),
            dma((nd, rd)),
            dma((nh, 3)),
            dma((nh, 3)),
            dma((n,)),
            dma((n,)),
            dma((nd, rd)),
            dma((nd, rd)),
            dma((nh, rd)),
            dma((nh, rd)),
        ],
        compiler_params=pltpu.CompilerParams(
            collective_id=0, has_side_effects=True, vmem_limit_bytes=56 * 1024 * 1024
        ),
    )(*operands)


def solution(mesh):
    nd = mesh.shape["dap"]
    nh = mesh.shape["head"]
    return jax.shard_map(
        functools.partial(per_device, nd, nh),
        mesh=mesh,
        in_specs=(
            P("dap", None, None),
            P(),
            P(),
            P(),
            P(),
            P(None, None, "head"),
            P("head"),
            P("head", None),
            P(),
            P(),
            P(),
            P(),
            P(),
            P(),
        ),
        out_specs=(P(("dap", "head"), None, None), P("dap", "head", None)),
        check_vma=False,
    )
```
